32 devices in a mesh: dp: 2 (over core), row: 4 (over y, x), col: 4 (over z).
Axes of the slice: x: 2, y: 2, z: 4, core: 2. Of those that a mesh axis runs over, the one named last changes fastest.
Arguments:
- block_input: bfloat16 [2048, 1024], P(('dp', 'row', 'col')), may hold values from -6 to 6
- seq_lengths: int32 [2, 5], P('dp'), may hold values from 1 to 512, 1024 in all within a row
- out_grad: bfloat16 [2048, 1024], P(('dp', 'row', 'col')), may hold values from -6 to 6
- attn_norm: float32 [1024], replicated, may hold values from 0.5 to 1.5
- query_weight: bfloat16 [1024, 1024], P('col', 'row'), may hold values from -0.1875 to 0.1875
- key_weight: bfloat16 [1024, 512], P('col', 'row'), may hold values from -0.1875 to 0.1875
- value_weight: bfloat16 [1024, 512], P('col', 'row'), may hold values from -0.1875 to 0.1875
- query_norm: float32 [64], replicated, may hold values from 0.5 to 1.5
- key_norm: float32 [64], replicated, may hold values from 0.5 to 1.5
- out_weight: bfloat16 [1024, 1024], P(('row', 'col')), may hold values from -0.75 to 0.75
- ffn_norm: float32 [1024], replicated, may hold values from 0.5 to 1.5
- gate_weight: bfloat16 [1024, 4608], P('col', 'row'), may hold values from -0.1875 to 0.1875
- up_weight: bfloat16 [1024, 4608], P('col', 'row'), may hold values from -0.1875 to 0.1875
- down_weight: bfloat16 [4608, 1024], P(('row', 'col')), may hold values from -0.09375 to 0.09375
Outputs:
- block_output: bfloat16 [2048, 1024], P(('dp', 'row', 'col'))
- input_grad: float32 [2048, 1024], P(('dp', 'row', 'col'))
- grad_attnnorm: float32 [1024], replicated
- grad_query: float32 [1024, 1024], P('col', 'row')
- grad_key: float32 [1024, 512], P('col', 'row')
- grad_value: float32 [1024, 512], P('col', 'row')
- grad_qnorm: float32 [64], replicated
- grad_knorm: float32 [64], replicated
- grad_outweight: float32 [1024, 1024], P(('row', 'col'))
- grad_ffnnorm: float32 [1024], replicated
- grad_gate: float32 [1024, 4608], P('col', 'row')
- grad_up: float32 [1024, 4608], P('col', 'row')
- grad_down: float32 [4608, 1024], P(('row', 'col'))
The draws below stay inside these ranges and needn't reach their ends.
Inputs may be any that keep to these rules, and one draw needn't show every extreme that they name: Each row of seq_lengths sums to 1024, and its largest entry is exactly 512.
All inputs are finite; a program needn't handle non-finite values.
Results may differ from the reference program's by a relative error of at most 0.012.
The reference program's roundings to bfloat16 on the way count: a program that leaves them out, or rounds other values in their place, can miss the bound.
Values may be sent and summed in bfloat16 or wider, within the bound.
A program may use at most 128 MiB of HBM per device.

```python
import math
import jax
import jax.numpy as jnp
import numpy as np
from jax import lax

D = 1024
H = 16
KV = 8
HD = 64
FF = 4608
MAXLEN = 512
T_DP = 1024
NSEQ = 5
TOKENS = 2048
QD = 1024
KD = 512
N_DP = 2


def block_scale(key, extent, pieces, least, top_value):
    factor_of, own = 1.0, jax.random.fold_in(key, 6)
    for dim, shards_of in pieces:
        draws = jnp.exp(jax.random.uniform(jax.random.fold_in(own, dim), (shards_of,), jnp.float32, least / len(pieces), top_value / len(pieces)))
        factor_of = factor_of * jnp.repeat(draws, extent[dim] // shards_of).reshape([-1 if axis == dim else 1 for axis in range(len(extent))])
    return factor_of


def profile(amount, total, most, slope):
    weights = [(1 << 20) // math.isqrt(grade ** slope) + 1 for grade in range(2, amount + 1)]
    rest, counts = total - most - (amount - 1), [1] * (amount - 1)
    while rest > 0:
        free = [i for i in range(amount - 1) if counts[i] < most]
        pool, remaining = sum([weights[i] for i in free]), rest
        for i in free:
            more = min(most - counts[i], max(1, remaining * weights[i] // pool), rest)
            counts[i] = counts[i] + more
            rest = rest - more
    return np.array([most] + counts)


def uneven_parts(own_key, amount, total, most, lean):
    if amount == 2:
        one = jax.random.randint(own_key, (), max(1, total - most), min(most, total - 1) + 1)
        return jnp.stack([one, total - one])
    tallies = jnp.asarray(profile(amount, total, most, lean), jnp.int32)
    pairs = (amount - 1) // 2
    source_of, receiver = tallies[1:1 + 2 * pairs:2], tallies[2:2 + 2 * pairs:2]
    margin = jnp.minimum(source_of - 1, most - receiver)
    shifted = jax.random.randint(jax.random.fold_in(own_key, 1), (pairs,), 0, 1 << 20) % (margin + 1)
    tallies = tallies.at[1:1 + 2 * pairs:2].set(source_of - shifted).at[2:2 + 2 * pairs:2].set(receiver + shifted)
    return tallies[jax.random.permutation(jax.random.fold_in(own_key, 2), amount)]


def noise(own_key, dims, spread, limit, shards=(), kind=jnp.bfloat16):
    drawn = jax.random.normal(own_key, dims, jnp.float32) * spread
    if len(shards) > 0:
        drawn = block_scale(own_key, dims, shards, -0.22, 0.18) * drawn
    return jnp.clip(drawn, min=-limit, max=limit).astype(kind)


def setup_inputs(seed: int = 0) -> dict:
    keys = jax.random.split(jax.random.key(seed), 15)
    return {
        "block_input": noise(keys[0], (TOKENS, D), 1.0, 6.0, ((0, 32),)),
        "seq_lengths": jax.vmap(lambda own: uneven_parts(own, NSEQ, T_DP, MAXLEN, 2))(jax.random.split(keys[1], N_DP)).reshape((N_DP, NSEQ)).astype(jnp.int32),
        "out_grad": noise(keys[2], (TOKENS, D), 1.0, 6.0, ((0, 32),)),
        "attn_norm": jnp.clip(1.0 + 0.1 * jax.random.normal(keys[3], (D,), jnp.float32), 0.5, 1.5),
        "query_weight": noise(keys[4], (D, QD), D ** -0.5, 0.1875, ((0, 4), (1, 4))),
        "key_weight": noise(keys[5], (D, KD), D ** -0.5, 0.1875, ((0, 4), (1, 4))),
        "value_weight": noise(keys[6], (D, KD), D ** -0.5, 0.1875, ((0, 4), (1, 4))),
        "query_norm": jnp.clip(1.0 + 0.1 * jax.random.normal(keys[7], (HD,), jnp.float32), 0.5, 1.5),
        "key_norm": jnp.clip(1.0 + 0.1 * jax.random.normal(keys[8], (HD,), jnp.float32), 0.5, 1.5),
        "out_weight": noise(keys[9], (QD, D), HD ** -0.5, 0.75, ((0, 16),)),
        "ffn_norm": jnp.clip(1.0 + 0.1 * jax.random.normal(keys[10], (D,), jnp.float32), 0.5, 1.5),
        "gate_weight": noise(keys[11], (D, FF), D ** -0.5, 0.1875, ((0, 4), (1, 4))),
        "up_weight": noise(keys[12], (D, FF), D ** -0.5, 0.1875, ((0, 4), (1, 4))),
        "down_weight": noise(keys[13], (FF, D), FF ** -0.5, 0.09375, ((0, 16),)),
    }


EPSILON = 1e-05
THETA = 1000000.0

def segment_info(seq_lengths, length):
    end_points = jnp.cumsum(seq_lengths).astype(jnp.int32)
    places = jnp.arange(length, dtype=jnp.int32)
    passed = (places[:, None] >= end_points[None, :]).astype(jnp.int32)
    segment = lax.optimization_barrier(jnp.sum(passed, axis=1)).astype(jnp.int32)
    begins = lax.optimization_barrier(jnp.sum(passed * seq_lengths[None, :], axis=1)).astype(jnp.int32)
    return (segment, places - begins)

def rope_tables(position, width):
    half_width = width // 2
    exponent = jnp.arange(half_width, dtype=jnp.float32) * (2.0 / width)
    frequency = jnp.exp(-math.log(THETA) * exponent)
    angles = position.astype(jnp.float32)[:, None] * frequency[None, :]
    return (jnp.cos(angles), jnp.sin(angles))

def rotate(values, cosine, sine):
    half_width = values.shape[-1] // 2
    first_half = values[:, :half_width]
    second_half = values[:, half_width:]
    return jnp.concatenate([first_half * cosine - second_half * sine, second_half * cosine + first_half * sine], axis=1)

def rotate_back(cotangent, cosine, sine):
    half_width = cotangent.shape[-1] // 2
    first_half = cotangent[:, :half_width]
    second_half = cotangent[:, half_width:]
    return jnp.concatenate([first_half * cosine + second_half * sine, second_half * cosine - first_half * sine], axis=1)

def head_norm(values, gain_vec):
    inv_rms = lax.rsqrt(lax.optimization_barrier(jnp.mean(values * values, axis=-1, keepdims=True)) + EPSILON)
    return (values * inv_rms * gain_vec, inv_rms)

def head_norm_back(cotangent, values, inv_rms, gain_vec):
    normed = values * inv_rms
    weighted = cotangent * gain_vec
    gain_grad = lax.optimization_barrier(jnp.sum(cotangent * normed, axis=0))
    inner_mean = lax.optimization_barrier(jnp.mean(weighted * normed, axis=-1, keepdims=True))
    return (inv_rms * (weighted - normed * inner_mean), gain_grad)

def attend(queries, key_rows, value_rows, segment):
    length = queries.shape[0]
    block_rows = min(512, length)
    places = jnp.arange(length, dtype=jnp.int32)
    score_scale = 1.0 / math.sqrt(queries.shape[1])

    def one_block(number):
        offset = number * block_rows
        query_block = lax.dynamic_slice_in_dim(queries, offset, block_rows, 0)
        row_segment = lax.dynamic_slice_in_dim(segment, offset, block_rows, 0)
        row_places = offset + jnp.arange(block_rows, dtype=jnp.int32)
        allowed = (row_segment[:, None] == segment[None, :]) & (places[None, :] <= row_places[:, None])
        scores = jnp.dot(query_block, key_rows.T, preferred_element_type=jnp.float32) * score_scale
        exponent = jnp.where(allowed, jnp.exp(scores), 0.0)
        log_total = jnp.log(lax.optimization_barrier(jnp.sum(exponent, axis=1)))
        probability = jnp.where(allowed, jnp.exp(scores - log_total[:, None]), 0.0).astype(jnp.bfloat16)
        output = jnp.dot(probability, value_rows, preferred_element_type=jnp.float32)
        return (output, log_total)
    outputs, totals = lax.map(one_block, jnp.arange(length // block_rows, dtype=jnp.int32))
    return (outputs.reshape(length, -1), totals.reshape(length))

def attend_back(queries, key_rows, value_rows, segment, output_rows, out_grads, log_total):
    length = queries.shape[0]
    block_rows = min(512, length)
    places = jnp.arange(length, dtype=jnp.int32)
    score_scale = 1.0 / math.sqrt(queries.shape[1])

    def one_block(carried, number):
        key_total, value_total = carried
        offset = number * block_rows
        query_block = lax.dynamic_slice_in_dim(queries, offset, block_rows, 0)
        row_segment = lax.dynamic_slice_in_dim(segment, offset, block_rows, 0)
        grad_block = lax.dynamic_slice_in_dim(out_grads, offset, block_rows, 0)
        out_block = lax.dynamic_slice_in_dim(output_rows, offset, block_rows, 0)
        total_block = lax.dynamic_slice_in_dim(log_total, offset, block_rows, 0)
        row_places = offset + jnp.arange(block_rows, dtype=jnp.int32)
        allowed = (row_segment[:, None] == segment[None, :]) & (places[None, :] <= row_places[:, None])
        scores = jnp.dot(query_block, key_rows.T, preferred_element_type=jnp.float32) * score_scale
        probability = jnp.where(allowed, jnp.exp(scores - total_block[:, None]), 0.0).astype(jnp.bfloat16)
        value_total = value_total + jnp.dot(probability.T, grad_block, preferred_element_type=jnp.float32)
        prob_grad = jnp.dot(grad_block, value_rows.T, preferred_element_type=jnp.float32)
        row_delta = lax.optimization_barrier(jnp.sum(grad_block.astype(jnp.float32) * out_block.astype(jnp.float32), axis=1, keepdims=True))
        score_grad = (score_scale * probability.astype(jnp.float32) * (prob_grad - row_delta)).astype(jnp.bfloat16)
        query_grad = jnp.dot(score_grad, key_rows, preferred_element_type=jnp.float32)
        key_total = key_total + jnp.dot(score_grad.T, query_block, preferred_element_type=jnp.float32)
        return ((key_total, value_total), query_grad)
    zero_rows = jnp.zeros((length, queries.shape[1]), jnp.float32)
    (key_grad, value_grad), query_grads = lax.scan(one_block, (zero_rows, zero_rows), jnp.arange(length // block_rows, dtype=jnp.int32))
    return (query_grads.reshape(length, -1), key_grad, value_grad)

def head_inputs(query_raw, key_raw, value_raw, query_norm, key_norm, cosine, sine):
    query_normed, query_scale = head_norm(query_raw, query_norm)
    key_normed, key_scale = head_norm(key_raw, key_norm)
    query_rot = rotate(query_normed, cosine, sine).astype(jnp.bfloat16)
    key_rot = rotate(key_normed, cosine, sine).astype(jnp.bfloat16)
    return (query_rot, key_rot, value_raw.astype(jnp.bfloat16), query_scale, key_scale)

def head_forward(query_raw, key_raw, value_raw, query_norm, key_norm, cosine, sine, segment):
    query_rot, key_rot, value_low, query_scale, key_scale = head_inputs(query_raw, key_raw, value_raw, query_norm, key_norm, cosine, sine)
    output, log_total = attend(query_rot, key_rot, value_low, segment)
    return (output.astype(jnp.bfloat16), log_total)

def head_backward(query_raw, key_raw, value_raw, query_norm, key_norm, cosine, sine, segment, attn_low, cat_grad, log_total):
    query_rot, key_rot, value_low, query_scale, key_scale = head_inputs(query_raw, key_raw, value_raw, query_norm, key_norm, cosine, sine)
    query_grad, key_grad, value_grad = attend_back(query_rot, key_rot, value_low, segment, attn_low, cat_grad, log_total)
    query_pre, query_gain = head_norm_back(rotate_back(query_grad, cosine, sine), query_raw, query_scale, query_norm)
    key_pre, key_gain = head_norm_back(rotate_back(key_grad, cosine, sine), key_raw, key_scale, key_norm)
    return (query_pre.astype(jnp.bfloat16), key_pre.astype(jnp.bfloat16), value_grad.astype(jnp.bfloat16), query_gain, key_gain)

def group_pass(group_input, group_lengths, group_grad, attn_norm, query_weight, key_weight, value_weight, query_norm, key_norm, out_weight, ffn_norm, gate_weight, up_weight, down_weight):
    length = group_input.shape[0]
    segment, position = segment_info(group_lengths, length)
    cosine, sine = rope_tables(position, HD)
    residual = group_input.astype(jnp.float32)
    normed_in, scale_in = head_norm(residual, attn_norm)
    first_act = normed_in.astype(jnp.bfloat16)
    query_all = jnp.dot(first_act, query_weight, preferred_element_type=jnp.float32).reshape(length, H, HD).transpose(1, 0, 2)
    key_all = jnp.dot(first_act, key_weight, preferred_element_type=jnp.float32).reshape(length, KV, HD).transpose(1, 0, 2)
    value_all = jnp.dot(first_act, value_weight, preferred_element_type=jnp.float32).reshape(length, KV, HD).transpose(1, 0, 2)
    key_rep = jnp.repeat(key_all, 2, axis=0)
    value_rep = jnp.repeat(value_all, 2, axis=0)

    def forward_head(head_item):
        return head_forward(head_item[0], head_item[1], head_item[2], query_norm, key_norm, cosine, sine, segment)
    attn_heads, log_totals = lax.map(forward_head, (query_all, key_rep, value_rep))
    attn_cat = attn_heads.transpose(1, 0, 2).reshape(length, H * HD)
    middle = residual + jnp.dot(attn_cat, out_weight, preferred_element_type=jnp.float32)
    normed_mid, scale_mid = head_norm(middle, ffn_norm)
    second_act = normed_mid.astype(jnp.bfloat16)
    gating = jnp.dot(second_act, gate_weight, preferred_element_type=jnp.float32)
    upward = jnp.dot(second_act, up_weight, preferred_element_type=jnp.float32)
    sigmoid_gate = jax.nn.sigmoid(gating)
    activated = gating * sigmoid_gate
    hidden = (activated * upward).astype(jnp.bfloat16)
    result_sum = middle + jnp.dot(hidden, down_weight, preferred_element_type=jnp.float32)
    group_output = result_sum.astype(jnp.bfloat16)
    grad_down = jnp.dot(hidden.T, group_grad, preferred_element_type=jnp.float32)
    hidden_grad = jnp.dot(group_grad, down_weight.T, preferred_element_type=jnp.float32)
    gate_low = (hidden_grad * upward * sigmoid_gate * (1.0 + gating * (1.0 - sigmoid_gate))).astype(jnp.bfloat16)
    up_low = (hidden_grad * activated).astype(jnp.bfloat16)
    grad_gate = jnp.dot(second_act.T, gate_low, preferred_element_type=jnp.float32)
    grad_up = jnp.dot(second_act.T, up_low, preferred_element_type=jnp.float32)
    act_grad2 = jnp.dot(gate_low, gate_weight.T, preferred_element_type=jnp.float32) + jnp.dot(up_low, up_weight.T, preferred_element_type=jnp.float32)
    middle_back, ffn_gain_grad = head_norm_back(act_grad2, middle, scale_mid, ffn_norm)
    middle_grad = group_grad.astype(jnp.float32) + middle_back
    middle_low = middle_grad.astype(jnp.bfloat16)
    grad_outweight = jnp.dot(attn_cat.T, middle_low, preferred_element_type=jnp.float32)
    cat_grad = jnp.dot(middle_low, out_weight.T, preferred_element_type=jnp.float32).astype(jnp.bfloat16)
    cat_heads = cat_grad.reshape(length, H, HD).transpose(1, 0, 2)

    def backward_head(head_item):
        return head_backward(head_item[0], head_item[1], head_item[2], query_norm, key_norm, cosine, sine, segment, head_item[3], head_item[4], head_item[5])
    query_low, key_low, value_low, query_gains, key_gains = lax.map(backward_head, (query_all, key_rep, value_rep, attn_heads, cat_heads, log_totals))
    query_cat = query_low.transpose(1, 0, 2).reshape(length, H * HD)
    key_even = key_low[0::2].transpose(1, 0, 2).reshape(length, KV * HD)
    key_odd = key_low[1::2].transpose(1, 0, 2).reshape(length, KV * HD)
    value_even = value_low[0::2].transpose(1, 0, 2).reshape(length, KV * HD)
    value_odd = value_low[1::2].transpose(1, 0, 2).reshape(length, KV * HD)
    grad_query = jnp.dot(first_act.T, query_cat, preferred_element_type=jnp.float32)
    grad_key = jnp.dot(first_act.T, key_even, preferred_element_type=jnp.float32) + jnp.dot(first_act.T, key_odd, preferred_element_type=jnp.float32)
    grad_value = jnp.dot(first_act.T, value_even, preferred_element_type=jnp.float32) + jnp.dot(first_act.T, value_odd, preferred_element_type=jnp.float32)
    act_grad1 = jnp.dot(query_cat, query_weight.T, preferred_element_type=jnp.float32)
    act_grad1 = act_grad1 + jnp.dot(key_even, key_weight.T, preferred_element_type=jnp.float32) + jnp.dot(key_odd, key_weight.T, preferred_element_type=jnp.float32)
    act_grad1 = act_grad1 + jnp.dot(value_even, value_weight.T, preferred_element_type=jnp.float32) + jnp.dot(value_odd, value_weight.T, preferred_element_type=jnp.float32)
    input_back, attn_gain_grad = head_norm_back(act_grad1, residual, scale_in, attn_norm)
    input_grad = middle_grad + input_back
    gradients = (attn_gain_grad, grad_query, grad_key, grad_value, lax.optimization_barrier(jnp.sum(query_gains, axis=0)), lax.optimization_barrier(jnp.sum(key_gains, axis=0)), grad_outweight, ffn_gain_grad, grad_gate, grad_up, grad_down)
    return (group_output, input_grad, gradients)

def reference(block_input, seq_lengths, out_grad, attn_norm, query_weight, key_weight, value_weight, query_norm, key_norm, out_weight, ffn_norm, gate_weight, up_weight, down_weight):
    groups = seq_lengths.shape[0]
    width = block_input.shape[1]
    inputs = block_input.reshape(groups, -1, width)
    cotangents = out_grad.reshape(groups, -1, width)
    weights = (attn_norm, query_weight, key_weight, value_weight, query_norm, key_norm, out_weight, ffn_norm, gate_weight, up_weight, down_weight)
    zero_grads = tuple((jnp.zeros(weight_item.shape, jnp.float32) for weight_item in weights))

    def scan_step(carried, group_item):
        group_output, input_grad, gradients = group_pass(group_item[0], group_item[1], group_item[2], attn_norm, query_weight, key_weight, value_weight, query_norm, key_norm, out_weight, ffn_norm, gate_weight, up_weight, down_weight)
        summed = tuple((carried_item + grad_item for carried_item, grad_item in zip(carried, gradients)))
        return (summed, (group_output, input_grad))
    totals, (outputs, input_grads) = lax.scan(scan_step, zero_grads, (inputs, seq_lengths, cotangents))
    return (outputs.reshape(-1, width), input_grads.reshape(-1, width), totals[0], totals[1], totals[2], totals[3], totals[4], totals[5], totals[6], totals[7], totals[8], totals[9], totals[10])
```

```python
import math

import jax
import jax.numpy as jnp
from jax import lax
from jax.experimental import pallas as pl
from jax.experimental.pallas import tpu as pltpu
from jax.sharding import PartitionSpec as P

EPSILON = 1e-05
THETA = 1000000.0


def segment_info(seq_lengths, length):
    end_points = jnp.cumsum(seq_lengths)
    places = jnp.arange(length, dtype=jnp.int32)
    passed = (places[:, None] >= end_points[None, :]).astype(jnp.int32)
    segment = jnp.sum(passed, axis=1)
    begins = jnp.sum(passed * seq_lengths[None, :], axis=1)
    return (segment, places - begins)


def rope_tables(position, width):
    half_width = width // 2
    exponent = jnp.arange(half_width, dtype=jnp.float32) * (2.0 / width)
    frequency = jnp.exp(-math.log(THETA) * exponent)
    angles = position.astype(jnp.float32)[:, None] * frequency[None, :]
    return (jnp.cos(angles), jnp.sin(angles))


def rotate(values, cosine, sine):
    half_width = values.shape[-1] // 2
    first_half = values[:, :half_width]
    second_half = values[:, half_width:]
    return jnp.concatenate(
        [first_half * cosine - second_half * sine, second_half * cosine + first_half * sine], axis=1
    )


def rotate_back(cotangent, cosine, sine):
    half_width = cotangent.shape[-1] // 2
    first_half = cotangent[:, :half_width]
    second_half = cotangent[:, half_width:]
    return jnp.concatenate(
        [first_half * cosine + second_half * sine, second_half * cosine - first_half * sine], axis=1
    )


def head_norm(values, gain_vec):
    inv_rms = lax.rsqrt(jnp.mean(values * values, axis=-1, keepdims=True) + EPSILON)
    return (values * inv_rms * gain_vec, inv_rms)


def head_norm_back(cotangent, values, inv_rms, gain_vec):
    normed = values * inv_rms
    weighted = cotangent * gain_vec
    gain_grad = jnp.sum(cotangent * normed, axis=0)
    inner_mean = jnp.mean(weighted * normed, axis=-1, keepdims=True)
    return (inv_rms * (weighted - normed * inner_mean), gain_grad)


def attend(queries, key_rows, value_rows, segment):
    length = queries.shape[0]
    block_rows = min(512, length)
    places = jnp.arange(length, dtype=jnp.int32)
    score_scale = 1.0 / math.sqrt(queries.shape[1])

    def one_block(number):
        offset = number * block_rows
        query_block = lax.dynamic_slice_in_dim(queries, offset, block_rows, 0)
        row_segment = lax.dynamic_slice_in_dim(segment, offset, block_rows, 0)
        row_places = offset + jnp.arange(block_rows, dtype=jnp.int32)
        allowed = (row_segment[:, None] == segment[None, :]) & (
            places[None, :] <= row_places[:, None]
        )
        scores = jnp.dot(query_block, key_rows.T, preferred_element_type=jnp.float32) * score_scale
        exponent = jnp.where(allowed, jnp.exp(scores), 0.0)
        log_total = jnp.log(jnp.sum(exponent, axis=1))
        probability = jnp.where(allowed, jnp.exp(scores - log_total[:, None]), 0.0).astype(
            jnp.bfloat16
        )
        output = jnp.dot(probability, value_rows, preferred_element_type=jnp.float32)
        return (output, log_total)

    outputs, totals = lax.map(one_block, jnp.arange(length // block_rows, dtype=jnp.int32))
    return (outputs.reshape(length, -1), totals.reshape(length))


def attend_back(queries, key_rows, value_rows, segment, output_rows, out_grads, log_total):
    length = queries.shape[0]
    block_rows = min(512, length)
    places = jnp.arange(length, dtype=jnp.int32)
    score_scale = 1.0 / math.sqrt(queries.shape[1])

    def one_block(carried, number):
        key_total, value_total = carried
        offset = number * block_rows
        query_block = lax.dynamic_slice_in_dim(queries, offset, block_rows, 0)
        row_segment = lax.dynamic_slice_in_dim(segment, offset, block_rows, 0)
        grad_block = lax.dynamic_slice_in_dim(out_grads, offset, block_rows, 0)
        out_block = lax.dynamic_slice_in_dim(output_rows, offset, block_rows, 0)
        total_block = lax.dynamic_slice_in_dim(log_total, offset, block_rows, 0)
        row_places = offset + jnp.arange(block_rows, dtype=jnp.int32)
        allowed = (row_segment[:, None] == segment[None, :]) & (
            places[None, :] <= row_places[:, None]
        )
        scores = jnp.dot(query_block, key_rows.T, preferred_element_type=jnp.float32) * score_scale
        probability = jnp.where(allowed, jnp.exp(scores - total_block[:, None]), 0.0).astype(
            jnp.bfloat16
        )
        value_total = value_total + jnp.dot(
            probability.T, grad_block, preferred_element_type=jnp.float32
        )
        prob_grad = jnp.dot(grad_block, value_rows.T, preferred_element_type=jnp.float32)
        row_delta = jnp.sum(
            grad_block.astype(jnp.float32) * out_block.astype(jnp.float32), axis=1, keepdims=True
        )
        score_grad = (
            score_scale * probability.astype(jnp.float32) * (prob_grad - row_delta)
        ).astype(jnp.bfloat16)
        query_grad = jnp.dot(score_grad, key_rows, preferred_element_type=jnp.float32)
        key_total = key_total + jnp.dot(
            score_grad.T, query_block, preferred_element_type=jnp.float32
        )
        return ((key_total, value_total), query_grad)

    zero_rows = jnp.zeros((length, queries.shape[1]), jnp.float32)
    (key_grad, value_grad), query_grads = lax.scan(
        one_block, (zero_rows, zero_rows), jnp.arange(length // block_rows, dtype=jnp.int32)
    )
    return (query_grads.reshape(length, -1), key_grad, value_grad)


def head_inputs(query_raw, key_raw, value_raw, query_norm, key_norm, cosine, sine):
    query_normed, query_scale = head_norm(query_raw, query_norm)
    key_normed, key_scale = head_norm(key_raw, key_norm)
    query_rot = rotate(query_normed, cosine, sine).astype(jnp.bfloat16)
    key_rot = rotate(key_normed, cosine, sine).astype(jnp.bfloat16)
    return (query_rot, key_rot, value_raw.astype(jnp.bfloat16), query_scale, key_scale)


def head_forward(query_raw, key_raw, value_raw, query_norm, key_norm, cosine, sine, segment):
    query_rot, key_rot, value_low, query_scale, key_scale = head_inputs(
        query_raw, key_raw, value_raw, query_norm, key_norm, cosine, sine
    )
    output, log_total = attend(query_rot, key_rot, value_low, segment)
    return (output.astype(jnp.bfloat16), log_total)


def head_backward(
    query_raw,
    key_raw,
    value_raw,
    query_norm,
    key_norm,
    cosine,
    sine,
    segment,
    attn_low,
    cat_grad,
    log_total,
):
    query_rot, key_rot, value_low, query_scale, key_scale = head_inputs(
        query_raw, key_raw, value_raw, query_norm, key_norm, cosine, sine
    )
    query_grad, key_grad, value_grad = attend_back(
        query_rot, key_rot, value_low, segment, attn_low, cat_grad, log_total
    )
    query_pre, query_gain = head_norm_back(
        rotate_back(query_grad, cosine, sine), query_raw, query_scale, query_norm
    )
    key_pre, key_gain = head_norm_back(
        rotate_back(key_grad, cosine, sine), key_raw, key_scale, key_norm
    )
    return (
        query_pre.astype(jnp.bfloat16),
        key_pre.astype(jnp.bfloat16),
        value_grad.astype(jnp.bfloat16),
        query_gain,
        key_gain,
    )


MESH = pl.DeviceIdType.MESH


def enter(axes):
    barrier = pltpu.get_barrier_semaphore()
    count = 0
    for axis in axes:
        size, own = lax.axis_size(axis), lax.axis_index(axis)
        for step in range(1, size):
            pl.semaphore_signal(
                barrier, inc=1, device_id={axis: lax.rem(own + step, size)}, device_id_type=MESH
            )
        count += size - 1
    pl.semaphore_wait(barrier, count)


def send(source, target, sems, place, axis, index):
    copy = pltpu.make_async_remote_copy(
        src_ref=source,
        dst_ref=target,
        send_sem=sems[0].at[place],
        recv_sem=sems[1].at[place],
        device_id={axis: index},
        device_id_type=MESH,
    )
    copy.start()
    return copy


def start_swaps(ins, outs, sems):
    cols, own = lax.axis_size("col"), lax.axis_index("col")
    copies = []
    for number in range(len(ins)):
        for step in range(1, cols):
            peer = lax.rem(own + step, cols)
            copies.append(
                send(ins[number].at[peer], outs[number].at[own], sems, (number, step), "col", peer)
            )
        outs[number][own] = ins[number][own]
    return copies


def call_kernel(body, args, outs, scratch, number):
    vmem = pl.BlockSpec(memory_space=pltpu.VMEM)
    return pl.pallas_call(
        body,
        out_shape=outs,
        in_specs=[vmem] * len(args),
        out_specs=[vmem] * len(outs),
        scratch_shapes=scratch,
        compiler_params=pltpu.CompilerParams(collective_id=number, has_side_effects=True),
    )(*args)


def dma(*shape):
    return [pltpu.SemaphoreType.DMA(shape), pltpu.SemaphoreType.DMA(shape)]


def exchange(gathers, swaps, number):
    rows, cols = lax.axis_size("row"), lax.axis_size("col")
    many, total = len(gathers), len(gathers) + len(swaps)

    def body(*refs):
        ins, outs = refs[:total], refs[total : 2 * total]
        sems, swap_sems = refs[2 * total : 2 * total + 2], refs[2 * total + 2 :]
        row, col = lax.axis_index("row"), lax.axis_index("col")
        enter(("row", "col"))
        across, copies = {}, []
        for item in range(many):
            for step in range(1, cols):
                across[item, step] = send(
                    ins[item],
                    outs[item].at[row, col],
                    sems,
                    (item, 0, step),
                    "col",
                    lax.rem(col + step, cols),
                )
        for item in range(many):
            for turn in range(1, rows):
                copies.append(
                    send(
                        ins[item],
                        outs[item].at[row, col],
                        sems,
                        (item, turn, 0),
                        "row",
                        lax.rem(row + turn, rows),
                    )
                )
        copies += start_swaps(ins[many:], outs[many:], swap_sems)
        for item in range(many):
            outs[item][row, col] = ins[item][...]
        for step in range(1, cols):
            origin = lax.rem(col + cols - step, cols)
            for item in range(many):
                across[item, step].wait()
                block = outs[item].at[row, origin]
                for turn in range(1, rows):
                    copies.append(
                        send(
                            block,
                            block,
                            sems,
                            (item, turn, step),
                            "row",
                            lax.rem(row + turn, rows),
                        )
                    )
        for copy in copies:
            copy.wait()

    outs = [jax.ShapeDtypeStruct((rows, cols) + g.shape, g.dtype) for g in gathers]
    outs += [jax.ShapeDtypeStruct(w.shape, w.dtype) for w in swaps]
    scratch = dma(many, rows, cols) + dma(max(len(swaps), 1), cols)
    return call_kernel(body, list(gathers) + list(swaps), outs, scratch, number)


def reduce_rows(partial_value, swaps, number):
    rows, cols = lax.axis_size("row"), lax.axis_size("col")
    local = partial_value.shape[0] // (rows * cols)
    width = partial_value.shape[1]
    shaped = partial_value.astype(jnp.bfloat16).reshape(rows, cols, local, width)
    many = len(swaps)

    def body(*refs):
        part, ins = refs[0], refs[1 : 1 + many]
        result, outs = refs[1 + many], refs[2 + many : 2 + 2 * many]
        first, staged, second = refs[2 + 2 * many : 5 + 2 * many]
        first_sems, second_sems = refs[5 + 2 * many : 7 + 2 * many], refs[7 + 2 * many : 9 + 2 * many]
        swap_sems = refs[9 + 2 * many :]
        row, col = lax.axis_index("row"), lax.axis_index("col")
        enter(("row", "col"))
        down, across = {}, []
        order = list(range(1, cols)) + [0]
        for step in order:
            block = lax.rem(col + step, cols)
            for turn in range(1, rows):
                peer = lax.rem(row + turn, rows)
                down[step, turn] = send(
                    part.at[peer, block],
                    first.at[turn, step],
                    first_sems,
                    (turn, step),
                    "row",
                    peer,
                )
        copies = start_swaps(ins, outs, swap_sems)
        for step in order:
            block = lax.rem(col + step, cols)
            summed = part[row, block].astype(jnp.float32)
            for turn in range(1, rows):
                down[step, turn].wait()
                summed = summed + first[turn, step].astype(jnp.float32)
            if step == 0:
                result[...] = summed
            else:
                staged[step] = summed.astype(jnp.bfloat16)
                across.append(
                    send(staged.at[step], second.at[step], second_sems, (step,), "col", block)
                )
        for step in range(1, cols):
            across[step - 1].wait()
            result[...] += second[step].astype(jnp.float32)
        for copy in copies:
            copy.wait()

    outs = [jax.ShapeDtypeStruct((local, width), jnp.float32)]
    outs += [jax.ShapeDtypeStruct(w.shape, w.dtype) for w in swaps]
    scratch = [
        pltpu.VMEM((rows, cols, local, width), jnp.bfloat16),
        pltpu.VMEM((cols, local, width), jnp.bfloat16),
        pltpu.VMEM((cols, local, width), jnp.bfloat16),
    ]
    scratch += dma(rows, cols) + dma(cols) + dma(max(many, 1), cols)
    return call_kernel(body, [shaped] + list(swaps), outs, scratch, number)


def last_sums(group_value, gains, number):
    sizes = [lax.axis_size(axis) for axis in ("dp", "row", "col")]

    def body(value, gain, value_out, gain_out, value_in, landed, held, *sems):
        value_sems, gain_sems = sems[:2], sems[2:]
        enter(("dp", "row", "col"))
        copies, groups = [], lax.axis_size("dp")
        me = lax.axis_index("dp")
        for step in range(1, groups):
            copies.append(
                send(
                    value,
                    value_in.at[step],
                    value_sems,
                    (step,),
                    "dp",
                    lax.rem(me + step, groups),
                )
            )
        held[0] = gain[...]
        for stage, axis in enumerate(("dp", "row", "col")):
            size, own = lax.axis_size(axis), lax.axis_index(axis)
            sent = [
                send(
                    held.at[stage],
                    landed.at[stage, step],
                    gain_sems,
                    (stage, step),
                    axis,
                    lax.rem(own + step, size),
                )
                for step in range(1, size)
            ]
            held[stage + 1] = held[stage]
            landed[stage, 0] = held[stage]
            for copy in sent:
                copy.wait()
            total = None
            for place in range(size):
                term = landed[stage, lax.rem(own - place + size, size)]
                total = term if total is None else total + term
            held[stage + 1] = total
        gain_out[...] = held[3]
        for copy in copies:
            copy.wait()
        total = value[...]
        for step in range(1, groups):
            total = total + value_in[step]
        value_out[...] = total

    outs = [jax.ShapeDtypeStruct(v.shape, jnp.float32) for v in (group_value, gains)]
    scratch = [
        pltpu.VMEM((sizes[0],) + group_value.shape, jnp.float32),
        pltpu.VMEM((3, max(sizes)) + gains.shape, jnp.float32),
        pltpu.VMEM((4,) + gains.shape, jnp.float32),
    ]
    scratch += dma(sizes[0]) + dma(3, max(sizes))
    return call_kernel(body, [group_value, gains], outs, scratch, number)


def dot(left, right, left_dim=1, right_dim=0):
    return lax.dot_general(
        left,
        right,
        (((left_dim,), (right_dim,)), ((), ())),
        preferred_element_type=jnp.float32,
    )


def shards(
    block_input,
    seq_lengths,
    out_grad,
    attn_norm,
    query_weight,
    key_weight,
    value_weight,
    query_norm,
    key_norm,
    out_weight,
    ffn_norm,
    gate_weight,
    up_weight,
    down_weight,
):
    local_rows, width = block_input.shape
    head_dim = query_norm.shape[0]
    col_width = query_weight.shape[0]
    cols = lax.axis_size("col")
    length = local_rows * cols * lax.axis_size("row")
    place = (lax.axis_index("row") * cols + lax.axis_index("col")) * local_rows

    def own_rows(values):
        return lax.dynamic_slice_in_dim(values, place, local_rows, 0)

    out_weight_full = lax.all_gather(out_weight, ("row", "col"), axis=0, tiled=True)
    out_full = lax.all_gather(out_grad, ("row", "col"), axis=0, tiled=True)

    query_slots = query_weight.reshape(col_width, cols, head_dim)
    key_slots = jnp.repeat(key_weight.reshape(col_width, cols // 2, head_dim), 2, axis=1)
    value_slots = jnp.repeat(value_weight.reshape(col_width, cols // 2, head_dim), 2, axis=1)
    slots = jnp.concatenate([query_slots, key_slots, value_slots], axis=2).transpose(1, 0, 2)
    hidden_width = gate_weight.shape[1] // cols
    wide = jnp.concatenate(
        [
            gate_weight.reshape(col_width, cols, hidden_width),
            up_weight.reshape(col_width, cols, hidden_width),
        ],
        axis=2,
    ).transpose(1, 0, 2)

    input_blocks, slot_blocks = exchange([block_input], [slots], 0)
    input_full = input_blocks.reshape(length, width).astype(jnp.float32)
    slot_weight = slot_blocks.reshape(width, 3 * head_dim)
    first_full = head_norm(input_full, attn_norm)[0].astype(jnp.bfloat16)
    residual = block_input.astype(jnp.float32)
    scale_in = head_norm(residual, attn_norm)[1]
    segment, position = segment_info(seq_lengths[0], length)
    cosine, sine = rope_tables(position, head_dim)
    own_sums = dot(first_full, slot_weight)
    query_raw = own_sums[:, :head_dim]
    key_raw = own_sums[:, head_dim : 2 * head_dim]
    value_raw = own_sums[:, 2 * head_dim :]
    attn_low, log_total = head_forward(
        query_raw, key_raw, value_raw, query_norm, key_norm, cosine, sine, segment
    )
    cat_blocks, wide_blocks = exchange([attn_low.T], [wide], 1)
    cat_full = cat_blocks.reshape(width, length)
    wide_weight = wide_blocks.reshape(width, 2 * hidden_width)
    middle = input_full + dot(cat_full, out_weight_full, 0, 0)
    normed_mid, scale_mid = head_norm(middle, ffn_norm)
    second_full = normed_mid.astype(jnp.bfloat16)
    wide_sums = dot(second_full, wide_weight)
    gating, upward = wide_sums[:, :hidden_width], wide_sums[:, hidden_width:]
    sigmoid_gate = jax.nn.sigmoid(gating)
    activated = gating * sigmoid_gate
    hidden = (activated * upward).astype(jnp.bfloat16)
    hidden_grad = dot(out_full, down_weight, 1, 1)
    gate_low = (hidden_grad * upward * sigmoid_gate * (1.0 + gating * (1.0 - sigmoid_gate))).astype(
        jnp.bfloat16
    )
    up_low = (hidden_grad * activated).astype(jnp.bfloat16)
    wide_low = jnp.concatenate([gate_low, up_low], axis=1)
    (act_grad2,) = reduce_rows(dot(wide_low, wide_weight, 1, 1), [], 2)
    down_sums = lax.psum_scatter(
        dot(hidden, down_weight), ("row", "col"), scatter_dimension=0, tiled=True
    )
    middle_own = own_rows(middle)
    block_output = (middle_own + down_sums).astype(jnp.bfloat16)
    grad_down = dot(hidden, out_full, 0, 0)
    wide_grad = dot(second_full, wide_low, 0, 0).astype(jnp.bfloat16)
    middle_back, ffn_gain_grad = head_norm_back(
        act_grad2, middle_own, own_rows(scale_mid), ffn_norm
    )
    middle_grad = out_grad.astype(jnp.float32) + middle_back
    middle_blocks, wide_grads = exchange(
        [middle_grad.astype(jnp.bfloat16)],
        [wide_grad.reshape(cols, col_width, 2 * hidden_width)],
        3,
    )
    middle_full = middle_blocks.reshape(length, width)
    grad_outweight = dot(attn_low, middle_full, 0, 0)
    cat_grad = dot(middle_full, out_weight, 1, 1).astype(jnp.bfloat16)
    wide_grads = wide_grads.astype(jnp.float32).transpose(1, 0, 2)
    grad_gate = wide_grads[:, :, :hidden_width].reshape(col_width, -1)
    grad_up = wide_grads[:, :, hidden_width:].reshape(col_width, -1)
    grad_outweight, grad_gate, grad_up, grad_down = lax.psum(
        (grad_outweight, grad_gate, grad_up, grad_down), "dp"
    )
    query_low, key_low, value_low, query_gain, key_gain = head_backward(
        query_raw,
        key_raw,
        value_raw,
        query_norm,
        key_norm,
        cosine,
        sine,
        segment,
        attn_low,
        cat_grad,
        log_total,
    )
    own_slot = jnp.concatenate([query_low, key_low, value_low], axis=1)
    slot_grad = dot(first_full, own_slot, 0, 0).astype(jnp.bfloat16)
    act_grad1, slot_grads = reduce_rows(
        dot(own_slot, slot_weight, 1, 1),
        [slot_grad.reshape(cols, col_width, 3 * head_dim)],
        4,
    )
    slot_grads = slot_grads.astype(jnp.float32)
    query_part = slot_grads[:, :, :head_dim].transpose(1, 0, 2).reshape(col_width, -1)
    pairs = slot_grads.reshape(cols // 2, 2, col_width, 3 * head_dim).sum(axis=1).transpose(1, 0, 2)
    key_part = pairs[:, :, head_dim : 2 * head_dim].reshape(col_width, -1)
    value_part = pairs[:, :, 2 * head_dim :].reshape(col_width, -1)
    input_back, attn_gain_grad = head_norm_back(act_grad1, residual, scale_in, attn_norm)
    input_grad = middle_grad + input_back
    head_gains = jnp.concatenate(
        [query_gain, key_gain, jnp.zeros((width - 2 * head_dim,), jnp.float32)]
    )
    gains = jnp.stack([attn_gain_grad, ffn_gain_grad, head_gains])
    gains = jnp.concatenate([gains, jnp.zeros((5, width), jnp.float32)], axis=0)
    group_sums, gain_sums = last_sums(
        jnp.concatenate([query_part, key_part, value_part], axis=1), gains, 5
    )
    query_width, key_width = query_part.shape[1], key_part.shape[1]
    return (
        block_output,
        input_grad,
        gain_sums[0],
        group_sums[:, :query_width],
        group_sums[:, query_width : query_width + key_width],
        group_sums[:, query_width + key_width :],
        gain_sums[2, :head_dim],
        gain_sums[2, head_dim : 2 * head_dim],
        grad_outweight,
        gain_sums[1],
        grad_gate,
        grad_up,
        grad_down,
    )


def solution(mesh):
    placed = (
        P(("dp", "row", "col"), None),
        P("dp", None),
        P(("dp", "row", "col"), None),
        P(),
        P("col", "row"),
        P("col", "row"),
        P("col", "row"),
        P(),
        P(),
        P(("row", "col"), None),
        P(),
        P("col", "row"),
        P("col", "row"),
        P(("row", "col"), None),
    )
    return jax.shard_map(
        shards,
        mesh=mesh,
        in_specs=placed,
        out_specs=(
            P(("dp", "row", "col"), None),
            P(("dp", "row", "col"), None),
            P(),
            P("col", "row"),
            P("col", "row"),
            P("col", "row"),
            P(),
            P(),
            P(("row", "col"), None),
            P(),
            P("col", "row"),
            P("col", "row"),
            P(("row", "col"), None),
        ),
        check_vma=False,
    )
```

```python
import functools
import math

import jax
import jax.numpy as jnp
from jax import lax
from jax.experimental import pallas as pl
from jax.experimental.pallas import tpu as pltpu
from jax.sharding import PartitionSpec as P

EPSILON = 1e-05
THETA = 1000000.0


def segment_info(seq_lengths, length):
    end_points = jnp.cumsum(seq_lengths)
    places = jnp.arange(length, dtype=jnp.int32)
    passed = (places[:, None] >= end_points[None, :]).astype(jnp.int32)
    segment = jnp.sum(passed, axis=1)
    begins = jnp.sum(passed * seq_lengths[None, :], axis=1)
    return (segment, places - begins)


def rope_tables(position, width):
    half_width = width // 2
    exponent = jnp.arange(half_width, dtype=jnp.float32) * (2.0 / width)
    frequency = jnp.exp(-math.log(THETA) * exponent)
    angles = position.astype(jnp.float32)[:, None] * frequency[None, :]
    return (jnp.cos(angles), jnp.sin(angles))


def head_norm(values, gain_vec):
    inv_rms = lax.rsqrt(jnp.mean(values * values, axis=-1, keepdims=True) + EPSILON)
    return (values * inv_rms * gain_vec, inv_rms)


def head_norm_back(cotangent, values, inv_rms, gain_vec):
    normed = values * inv_rms
    weighted = cotangent * gain_vec
    gain_grad = jnp.sum(cotangent * normed, axis=0)
    inner_mean = jnp.mean(weighted * normed, axis=-1, keepdims=True)
    return (inv_rms * (weighted - normed * inner_mean), gain_grad)


def swap_halves(values):
    half_width = values.shape[-1] // 2
    return jnp.concatenate([values[:, half_width:], values[:, :half_width]], axis=1)


def block_probability(query_block, key_rows, begins, offset, low, shift):
    score_scale = 1.0 / math.sqrt(query_block.shape[1])
    scores = dot(query_block, key_rows, 1, 1) * score_scale
    places = low + lax.broadcasted_iota(jnp.int32, scores.shape, 1)
    row_places = offset + lax.broadcasted_iota(jnp.int32, scores.shape, 0)
    allowed = (places >= begins) & (places <= row_places)
    if shift is None:
        shift = jnp.log(jnp.sum(jnp.where(allowed, jnp.exp(scores), 0.0), axis=1, keepdims=True))
    probability = jnp.where(allowed, jnp.exp(scores - shift), 0.0).astype(jnp.bfloat16)
    return probability, shift


def spans(length, longest):
    block = min(256, length)
    return [
        (offset, max(0, (offset - longest) // 128 * 128), block)
        for offset in range(0, length, block)
    ]


def attend_kernel(longest, sums, gains, cosine, sine, begins, *outs):
    query_rot, key_rot, value_low, low_rows, low_cols, totals = outs
    length, head_dim = query_rot.shape
    for place, target in ((0, query_rot), (1, key_rot)):
        normed = head_norm(
            sums[:, place * head_dim : (place + 1) * head_dim], gains[place : place + 1, :]
        )[0]
        target[...] = (normed * cosine[...] + swap_halves(normed) * sine[...]).astype(jnp.bfloat16)
    value_low[...] = sums[:, 2 * head_dim : 3 * head_dim].astype(jnp.bfloat16)
    for offset, low, block in spans(length, longest):
        rows, keys = slice(offset, offset + block), slice(low, offset + block)
        probability, total = block_probability(
            query_rot[rows, :], key_rot[keys, :], begins[rows, :], offset, low, None
        )
        totals[rows, :] = total
        low_rows[rows, :] = dot(probability, value_low[keys, :]).astype(jnp.bfloat16)
        low_cols[:, rows] = dot(value_low[keys, :], probability, 0, 1).astype(jnp.bfloat16)


def attend_back_kernel(longest, *refs):
    query_rot, key_rot, value_low, low_rows, totals, grads = refs[:6]
    sums, gains, cosine, sine, begins = refs[6:11]
    slot, gain_out, query_acc, key_acc, value_acc = refs[11:]
    length, head_dim = query_rot.shape
    score_scale = 1.0 / math.sqrt(head_dim)
    key_acc[...] = jnp.zeros_like(key_acc)
    value_acc[...] = jnp.zeros_like(value_acc)
    for offset, low, block in spans(length, longest):
        rows, keys = slice(offset, offset + block), slice(low, offset + block)
        probability, _ = block_probability(
            query_rot[rows, :], key_rot[keys, :], begins[rows, :], offset, low, totals[rows, :]
        )
        grad_block = grads[rows, :]
        value_acc[keys, :] += dot(probability, grad_block, 0, 0)
        row_delta = jnp.sum(
            grad_block.astype(jnp.float32) * low_rows[rows, :].astype(jnp.float32),
            axis=1,
            keepdims=True,
        )
        prob_grad = dot(grad_block, value_low[keys, :], 1, 1)
        score_grad = (
            score_scale * probability.astype(jnp.float32) * (prob_grad - row_delta)
        ).astype(jnp.bfloat16)
        query_acc[rows, :] = dot(score_grad, key_rot[keys, :])
        key_acc[keys, :] += dot(score_grad, query_rot[rows, :], 0, 0)
    parts = []
    for place, source in ((0, query_acc), (1, key_acc)):
        raw = sums[:, place * head_dim : (place + 1) * head_dim]
        gain = gains[place : place + 1, :]
        inv_rms = head_norm(raw, gain)[1]
        cotangent = source[...] * cosine[...] - swap_halves(source[...]) * sine[...]
        low_part, gain_grad = head_norm_back(cotangent, raw, inv_rms, gain)
        parts.append(low_part.astype(jnp.bfloat16))
        gain_out[place : place + 1, :] = gain_grad[None, :]
    parts.append(value_acc[...].astype(jnp.bfloat16))
    for place in range(3):
        slot[:, place * head_dim : (place + 1) * head_dim] = parts[place]


def local_kernel(body, args, outs, scratch=()):
    vmem = pl.BlockSpec(memory_space=pltpu.VMEM)
    return pl.pallas_call(
        body,
        out_shape=outs,
        in_specs=[vmem] * len(args),
        out_specs=[vmem] * len(outs),
        scratch_shapes=list(scratch),
    )(*args)


def pack_slots_kernel(cols, head_dim, query, key, value, out):
    for col in range(cols):
        half = col // 2
        out[col, :, :head_dim] = query[:, col * head_dim : (col + 1) * head_dim]
        for place, source in ((1, key), (2, value)):
            out[col, :, place * head_dim : (place + 1) * head_dim] = source[
                :, half * head_dim : (half + 1) * head_dim
            ]


def pack_wide_kernel(cols, gate, up, out):
    part = gate.shape[1] // cols
    for col in range(cols):
        out[col, :, :part] = gate[:, col * part : (col + 1) * part]
        out[col, :, part:] = up[:, col * part : (col + 1) * part]


def open_wide_kernel(cols, wide, gate, up):
    part = gate.shape[1] // cols
    for col in range(cols):
        gate[:, col * part : (col + 1) * part] = wide[col, :, :part].astype(jnp.float32)
        up[:, col * part : (col + 1) * part] = wide[col, :, part:].astype(jnp.float32)


def open_slots_kernel(cols, head_dim, slots, out):
    for col in range(cols):
        out[:, col * head_dim : (col + 1) * head_dim] = slots[col, :, :head_dim].astype(jnp.float32)
    for half in range(cols // 2):
        for place in (1, 2):
            lanes = slice(place * head_dim, (place + 1) * head_dim)
            begin = (cols + (place - 1) * (cols // 2) + half) * head_dim
            out[:, begin : begin + head_dim] = slots[2 * half, :, lanes].astype(
                jnp.float32
            ) + slots[2 * half + 1, :, lanes].astype(jnp.float32)


MESH = pl.DeviceIdType.MESH


def enter(axes):
    barrier = pltpu.get_barrier_semaphore()
    count = 0
    for axis in axes:
        size, own = lax.axis_size(axis), lax.axis_index(axis)
        for step in range(1, size):
            pl.semaphore_signal(
                barrier, inc=1, device_id={axis: lax.rem(own + step, size)}, device_id_type=MESH
            )
        count += size - 1
    pl.semaphore_wait(barrier, count)


def send(source, target, sems, place, axis, index):
    copy = pltpu.make_async_remote_copy(
        src_ref=source,
        dst_ref=target,
        send_sem=sems[0].at[place],
        recv_sem=sems[1].at[place],
        device_id={axis: index},
        device_id_type=MESH,
    )
    copy.start()
    return copy


def start_swaps(ins, outs, sems):
    cols, own = lax.axis_size("col"), lax.axis_index("col")
    copies = []
    for number in range(len(ins)):
        for step in range(1, cols):
            peer = lax.rem(own + step, cols)
            copies.append(
                send(ins[number].at[peer], outs[number].at[own], sems, (number, step), "col", peer)
            )
        outs[number][own] = ins[number][own]
    return copies


def call_kernel(body, args, outs, scratch, number):
    vmem = pl.BlockSpec(memory_space=pltpu.VMEM)
    return pl.pallas_call(
        body,
        out_shape=outs,
        in_specs=[vmem] * len(args),
        out_specs=[vmem] * len(outs),
        scratch_shapes=scratch,
        compiler_params=pltpu.CompilerParams(collective_id=number, has_side_effects=True),
    )(*args)


def dma(*shape):
    return [pltpu.SemaphoreType.DMA(shape), pltpu.SemaphoreType.DMA(shape)]


def exchange(gathers, swaps, number):
    rows, cols = lax.axis_size("row"), lax.axis_size("col")
    many, total = len(gathers), len(gathers) + len(swaps)

    def body(*refs):
        ins, outs = refs[:total], refs[total : 2 * total]
        sems, swap_sems = refs[2 * total : 2 * total + 2], refs[2 * total + 2 :]
        row, col = lax.axis_index("row"), lax.axis_index("col")
        enter(("row", "col"))
        across, copies = {}, []
        for item in range(many):
            for step in range(1, cols):
                across[item, step] = send(
                    ins[item],
                    outs[item].at[row, col],
                    sems,
                    (item, 0, step),
                    "col",
                    lax.rem(col + step, cols),
                )
        for item in range(many):
            for turn in range(1, rows):
                copies.append(
                    send(
                        ins[item],
                        outs[item].at[row, col],
                        sems,
                        (item, turn, 0),
                        "row",
                        lax.rem(row + turn, rows),
                    )
                )
        copies += start_swaps(ins[many:], outs[many:], swap_sems)
        for item in range(many):
            outs[item][row, col] = ins[item][...]
        for step in range(1, cols):
            origin = lax.rem(col + cols - step, cols)
            for item in range(many):
                across[item, step].wait()
                block = outs[item].at[row, origin]
                for turn in range(1, rows):
                    copies.append(
                        send(
                            block,
                            block,
                            sems,
                            (item, turn, step),
                            "row",
                            lax.rem(row + turn, rows),
                        )
                    )
        for copy in copies:
            copy.wait()

    outs = [jax.ShapeDtypeStruct((rows, cols) + g.shape, g.dtype) for g in gathers]
    outs += [jax.ShapeDtypeStruct(w.shape, w.dtype) for w in swaps]
    scratch = dma(many, rows, cols) + dma(max(len(swaps), 1), cols)
    return call_kernel(body, list(gathers) + list(swaps), outs, scratch, number)


def reduce_rows(partial_value, swaps, number):
    rows, cols = lax.axis_size("row"), lax.axis_size("col")
    local = partial_value.shape[0] // (rows * cols)
    width = partial_value.shape[1]
    shaped = partial_value.astype(jnp.bfloat16).reshape(rows, cols, local, width)
    many = len(swaps)

    def body(*refs):
        part, ins = refs[0], refs[1 : 1 + many]
        result, outs = refs[1 + many], refs[2 + many : 2 + 2 * many]
        first, staged, second = refs[2 + 2 * many : 5 + 2 * many]
        first_sems, second_sems = refs[5 + 2 * many : 7 + 2 * many], refs[7 + 2 * many : 9 + 2 * many]
        swap_sems = refs[9 + 2 * many :]
        row, col = lax.axis_index("row"), lax.axis_index("col")
        enter(("row", "col"))
        down, across = {}, []
        order = list(range(1, cols)) + [0]
        for step in order:
            block = lax.rem(col + step, cols)
            for turn in range(1, rows):
                peer = lax.rem(row + turn, rows)
                down[step, turn] = send(
                    part.at[peer, block],
                    first.at[turn, step],
                    first_sems,
                    (turn, step),
                    "row",
                    peer,
                )
        copies = start_swaps(ins, outs, swap_sems)
        for step in order:
            block = lax.rem(col + step, cols)
            summed = part[row, block].astype(jnp.float32)
            for turn in range(1, rows):
                down[step, turn].wait()
                summed = summed + first[turn, step].astype(jnp.float32)
            if step == 0:
                result[...] = summed
            else:
                staged[step] = summed.astype(jnp.bfloat16)
                across.append(
                    send(staged.at[step], second.at[step], second_sems, (step,), "col", block)
                )
        for step in range(1, cols):
            across[step - 1].wait()
            result[...] += second[step].astype(jnp.float32)
        for copy in copies:
            copy.wait()

    outs = [jax.ShapeDtypeStruct((local, width), jnp.float32)]
    outs += [jax.ShapeDtypeStruct(w.shape, w.dtype) for w in swaps]
    scratch = [
        pltpu.VMEM((rows, cols, local, width), jnp.bfloat16),
        pltpu.VMEM((cols, local, width), jnp.bfloat16),
        pltpu.VMEM((cols, local, width), jnp.bfloat16),
    ]
    scratch += dma(rows, cols) + dma(cols) + dma(max(many, 1), cols)
    return call_kernel(body, [shaped] + list(swaps), outs, scratch, number)


def last_sums(group_value, widths, gains, number):
    sizes = [lax.axis_size(axis) for axis in ("dp", "row", "col")]

    def body(value, gain, *refs):
        value_outs, gain_out = refs[: len(widths)], refs[len(widths)]
        value_in, landed, held = refs[len(widths) + 1 : len(widths) + 4]
        sems = refs[len(widths) + 4 :]
        value_sems, gain_sems = sems[:2], sems[2:]
        enter(("dp", "row", "col"))
        copies, groups = [], lax.axis_size("dp")
        me = lax.axis_index("dp")
        for step in range(1, groups):
            copies.append(
                send(
                    value,
                    value_in.at[step],
                    value_sems,
                    (step,),
                    "dp",
                    lax.rem(me + step, groups),
                )
            )
        held[0] = gain[...]
        for stage, axis in enumerate(("dp", "row", "col")):
            size, own = lax.axis_size(axis), lax.axis_index(axis)
            sent = [
                send(
                    held.at[stage],
                    landed.at[stage, step],
                    gain_sems,
                    (stage, step),
                    axis,
                    lax.rem(own + step, size),
                )
                for step in range(1, size)
            ]
            landed[stage, 0] = held[stage]
            for copy in sent:
                copy.wait()
            total = None
            for place in range(size):
                term = landed[stage, lax.rem(own - place + size, size)]
                total = term if total is None else total + term
            held[stage + 1] = total
        gain_out[...] = held[3]
        for copy in copies:
            copy.wait()
        total = value[...]
        for step in range(1, groups):
            total = total + value_in[step]
        begin = 0
        for size, value_out in zip(widths, value_outs):
            value_out[...] = total[:, begin : begin + size]
            begin += size

    outs = [jax.ShapeDtypeStruct((group_value.shape[0], size), jnp.float32) for size in widths]
    outs.append(jax.ShapeDtypeStruct(gains.shape, jnp.float32))
    scratch = [
        pltpu.VMEM((sizes[0],) + group_value.shape, jnp.float32),
        pltpu.VMEM((3, max(sizes)) + gains.shape, jnp.float32),
        pltpu.VMEM((4,) + gains.shape, jnp.float32),
    ]
    scratch += dma(sizes[0]) + dma(3, max(sizes))
    return call_kernel(body, [group_value, gains], outs, scratch, number)


def dot(left, right, left_dim=1, right_dim=0):
    return lax.dot_general(
        left,
        right,
        (((left_dim,), (right_dim,)), ((), ())),
        preferred_element_type=jnp.float32,
    )


def shards(
    block_input,
    seq_lengths,
    out_grad,
    attn_norm,
    query_weight,
    key_weight,
    value_weight,
    query_norm,
    key_norm,
    out_weight,
    ffn_norm,
    gate_weight,
    up_weight,
    down_weight,
):
    local_rows, width = block_input.shape
    head_dim = query_norm.shape[0]
    col_width = query_weight.shape[0]
    cols = lax.axis_size("col")
    length = local_rows * cols * lax.axis_size("row")
    place = (lax.axis_index("row") * cols + lax.axis_index("col")) * local_rows

    def own_rows(values):
        return lax.dynamic_slice_in_dim(values, place, local_rows, 0)

    out_weight_full = lax.all_gather(out_weight, ("row", "col"), axis=0, tiled=True)
    out_full = lax.all_gather(out_grad, ("row", "col"), axis=0, tiled=True)

    hidden_width = gate_weight.shape[1] // cols
    (slots,) = local_kernel(
        functools.partial(pack_slots_kernel, cols, head_dim),
        [query_weight, key_weight, value_weight],
        [jax.ShapeDtypeStruct((cols, col_width, 3 * head_dim), jnp.bfloat16)],
    )
    (wide,) = local_kernel(
        functools.partial(pack_wide_kernel, cols),
        [gate_weight, up_weight],
        [jax.ShapeDtypeStruct((cols, col_width, 2 * hidden_width), jnp.bfloat16)],
    )

    input_blocks, slot_blocks = exchange([block_input], [slots], 0)
    input_full = input_blocks.reshape(length, width).astype(jnp.float32)
    slot_weight = slot_blocks.reshape(width, 3 * head_dim)
    first_full = head_norm(input_full, attn_norm)[0].astype(jnp.bfloat16)
    residual = block_input.astype(jnp.float32)
    scale_in = head_norm(residual, attn_norm)[1]
    places = jnp.arange(length, dtype=jnp.int32)
    position = segment_info(seq_lengths[0], length)[1]
    begins = (places - position)[:, None]
    cosine, sine = rope_tables(position, head_dim)
    cosine = jnp.concatenate([cosine, cosine], axis=1)
    sine = jnp.concatenate([-sine, sine], axis=1)
    own_sums = dot(first_full, slot_weight)
    longest = length // 2
    head_gains = jnp.stack([query_norm, key_norm])
    row_shape = jax.ShapeDtypeStruct((length, head_dim), jnp.bfloat16)
    query_rot, key_rot, value_low, attn_low, attn_cols, log_total = local_kernel(
        functools.partial(attend_kernel, longest),
        [own_sums, head_gains, cosine, sine, begins],
        [
            row_shape,
            row_shape,
            row_shape,
            row_shape,
            jax.ShapeDtypeStruct((head_dim, length), jnp.bfloat16),
            jax.ShapeDtypeStruct((length, 1), jnp.float32),
        ],
    )
    cat_blocks, wide_blocks = exchange([attn_cols], [wide], 1)
    cat_full = cat_blocks.reshape(width, length)
    wide_weight = wide_blocks.reshape(width, 2 * hidden_width)
    middle = input_full + dot(cat_full, out_weight_full, 0, 0)
    normed_mid, scale_mid = head_norm(middle, ffn_norm)
    second_full = normed_mid.astype(jnp.bfloat16)
    wide_sums = dot(second_full, wide_weight)
    gating, upward = wide_sums[:, :hidden_width], wide_sums[:, hidden_width:]
    sigmoid_gate = jax.nn.sigmoid(gating)
    activated = gating * sigmoid_gate
    hidden = (activated * upward).astype(jnp.bfloat16)
    hidden_grad = dot(out_full, down_weight, 1, 1)
    gate_low = (hidden_grad * upward * sigmoid_gate * (1.0 + gating * (1.0 - sigmoid_gate))).astype(
        jnp.bfloat16
    )
    up_low = (hidden_grad * activated).astype(jnp.bfloat16)
    wide_low = jnp.concatenate([gate_low, up_low], axis=1)
    (act_grad2,) = reduce_rows(dot(wide_low, wide_weight, 1, 1), [], 2)
    down_part = dot(hidden, down_weight).astype(jnp.bfloat16)
    middle_own = own_rows(middle)
    grad_down = dot(hidden, out_full, 0, 0)
    wide_grad = dot(second_full, wide_low, 0, 0).astype(jnp.bfloat16)
    middle_back, ffn_gain_grad = head_norm_back(
        act_grad2, middle_own, own_rows(scale_mid), ffn_norm
    )
    middle_grad = out_grad.astype(jnp.float32) + middle_back
    middle_blocks, wide_grads = exchange(
        [middle_grad.astype(jnp.bfloat16)],
        [wide_grad.reshape(cols, col_width, 2 * hidden_width)],
        3,
    )
    middle_full = middle_blocks.reshape(length, width)
    grad_outweight = dot(attn_low, middle_full, 0, 0)
    cat_grad = dot(middle_full, out_weight, 1, 1).astype(jnp.bfloat16)
    wide_shape = jax.ShapeDtypeStruct(gate_weight.shape, jnp.float32)
    grad_gate, grad_up = local_kernel(
        functools.partial(open_wide_kernel, cols), [wide_grads], [wide_shape, wide_shape]
    )
    down_part, cat_grad = lax.optimization_barrier((down_part, cat_grad))
    down_sums = lax.psum_scatter(
        down_part, ("row", "col"), scatter_dimension=0, tiled=True
    ).astype(jnp.float32)
    block_output = (middle_own + down_sums).astype(jnp.bfloat16)
    accumulator = pltpu.VMEM((length, head_dim), jnp.float32)
    own_slot, head_gain_grads = local_kernel(
        functools.partial(attend_back_kernel, longest),
        [query_rot, key_rot, value_low, attn_low, log_total, cat_grad]
        + [own_sums, head_gains, cosine, sine, begins],
        [
            jax.ShapeDtypeStruct((length, 3 * head_dim), jnp.bfloat16),
            jax.ShapeDtypeStruct((2, head_dim), jnp.float32),
        ],
        [accumulator] * 3,
    )
    own_slot, grad_outweight, grad_down = lax.optimization_barrier(
        (own_slot, grad_outweight, grad_down)
    )
    grad_outweight, grad_gate, grad_up, grad_down = lax.psum(
        (grad_outweight, grad_gate, grad_up, grad_down), "dp"
    )
    slot_grad = dot(first_full, own_slot, 0, 0).astype(jnp.bfloat16)
    act_grad1, slot_grads = reduce_rows(
        dot(own_slot, slot_weight, 1, 1),
        [slot_grad.reshape(cols, col_width, 3 * head_dim)],
        4,
    )
    widths = (cols * head_dim, cols // 2 * head_dim, cols // 2 * head_dim)
    (slot_sums,) = local_kernel(
        functools.partial(open_slots_kernel, cols, head_dim),
        [slot_grads],
        [jax.ShapeDtypeStruct((col_width, sum(widths)), jnp.float32)],
    )
    input_back, attn_gain_grad = head_norm_back(act_grad1, residual, scale_in, attn_norm)
    input_grad = middle_grad + input_back
    flat_gains = jnp.concatenate(
        [head_gain_grads.reshape(-1), jnp.zeros((width - 2 * head_dim,), jnp.float32)]
    )
    gains = jnp.stack([attn_gain_grad, ffn_gain_grad, flat_gains])
    gains = jnp.concatenate([gains, jnp.zeros((5, width), jnp.float32)], axis=0)
    grad_query, grad_key, grad_value, gain_sums = last_sums(slot_sums, widths, gains, 5)
    return (
        block_output,
        input_grad,
        gain_sums[0],
        grad_query,
        grad_key,
        grad_value,
        gain_sums[2, :head_dim],
        gain_sums[2, head_dim : 2 * head_dim],
        grad_outweight,
        gain_sums[1],
        grad_gate,
        grad_up,
        grad_down,
    )


def solution(mesh):
    placed = (
        P(("dp", "row", "col"), None),
        P("dp", None),
        P(("dp", "row", "col"), None),
        P(),
        P("col", "row"),
        P("col", "row"),
        P("col", "row"),
        P(),
        P(),
        P(("row", "col"), None),
        P(),
        P("col", "row"),
        P("col", "row"),
        P(("row", "col"), None),
    )
    return jax.shard_map(
        shards,
        mesh=mesh,
        in_specs=placed,
        out_specs=(
            P(("dp", "row", "col"), None),
            P(("dp", "row", "col"), None),
            P(),
            P("col", "row"),
            P("col", "row"),
            P("col", "row"),
            P(),
            P(),
            P(("row", "col"), None),
            P(),
            P("col", "row"),
            P("col", "row"),
            P(("row", "col"), None),
        ),
        check_vma=False,
    )
```

```python
import functools
import math

import jax
import jax.numpy as jnp
from jax import lax
from jax.experimental import pallas as pl
from jax.experimental.pallas import tpu as pltpu
from jax.sharding import PartitionSpec as P

EPSILON = 1e-05
THETA = 1000000.0


def segment_info(seq_lengths, length):
    end_points = jnp.cumsum(seq_lengths)
    places = jnp.arange(length, dtype=jnp.int32)
    passed = (places[:, None] >= end_points[None, :]).astype(jnp.int32)
    segment = jnp.sum(passed, axis=1)
    begins = jnp.sum(passed * seq_lengths[None, :], axis=1)
    return (segment, places - begins)


def rope_tables(position, width):
    half_width = width // 2
    exponent = jnp.arange(half_width, dtype=jnp.float32) * (2.0 / width)
    frequency = jnp.exp(-math.log(THETA) * exponent)
    angles = position.astype(jnp.float32)[:, None] * frequency[None, :]
    return (jnp.cos(angles), jnp.sin(angles))


def head_norm(values, gain_vec):
    inv_rms = lax.rsqrt(jnp.mean(values * values, axis=-1, keepdims=True) + EPSILON)
    return (values * inv_rms * gain_vec, inv_rms)


def head_norm_back(cotangent, values, inv_rms, gain_vec):
    normed = values * inv_rms
    weighted = cotangent * gain_vec
    gain_grad = jnp.sum(cotangent * normed, axis=0)
    inner_mean = jnp.mean(weighted * normed, axis=-1, keepdims=True)
    return (inv_rms * (weighted - normed * inner_mean), gain_grad)


def swap_halves(values):
    half_width = values.shape[-1] // 2
    return jnp.concatenate([values[:, half_width:], values[:, :half_width]], axis=1)


def block_probability(query_block, key_rows, begins, offset, low, shift):
    score_scale = 1.0 / math.sqrt(query_block.shape[1])
    scores = dot(query_block, key_rows, 1, 1) * score_scale
    places = low + lax.broadcasted_iota(jnp.int32, scores.shape, 1)
    row_places = offset + lax.broadcasted_iota(jnp.int32, scores.shape, 0)
    allowed = (places >= begins) & (places <= row_places)
    if shift is None:
        shift = jnp.log(jnp.sum(jnp.where(allowed, jnp.exp(scores), 0.0), axis=1, keepdims=True))
    probability = jnp.where(allowed, jnp.exp(scores - shift), 0.0).astype(jnp.bfloat16)
    return probability, shift


def spans(length, longest):
    block = min(256, length)
    return [
        (offset, max(0, (offset - longest) // 128 * 128), block)
        for offset in range(0, length, block)
    ]


def attend_kernel(longest, sums, gains, cosine, sine, begins, *outs):
    query_rot, key_rot, value_low, low_rows, low_cols, totals = outs
    length, head_dim = query_rot.shape
    for place, target in ((0, query_rot), (1, key_rot)):
        normed = head_norm(
            sums[:, place * head_dim : (place + 1) * head_dim], gains[place : place + 1, :]
        )[0]
        target[...] = (normed * cosine[...] + swap_halves(normed) * sine[...]).astype(jnp.bfloat16)
    value_low[...] = sums[:, 2 * head_dim : 3 * head_dim].astype(jnp.bfloat16)
    for offset, low, block in spans(length, longest):
        rows, keys = slice(offset, offset + block), slice(low, offset + block)
        probability, total = block_probability(
            query_rot[rows, :], key_rot[keys, :], begins[rows, :], offset, low, None
        )
        totals[rows, :] = total
        low_rows[rows, :] = dot(probability, value_low[keys, :]).astype(jnp.bfloat16)
        low_cols[:, rows] = dot(value_low[keys, :], probability, 0, 1).astype(jnp.bfloat16)


def attend_back_kernel(longest, *refs):
    query_rot, key_rot, value_low, low_rows, totals, grads = refs[:6]
    sums, gains, cosine, sine, begins = refs[6:11]
    slot, gain_out, query_acc, key_acc, value_acc = refs[11:]
    length, head_dim = query_rot.shape
    score_scale = 1.0 / math.sqrt(head_dim)
    key_acc[...] = jnp.zeros_like(key_acc)
    value_acc[...] = jnp.zeros_like(value_acc)
    for offset, low, block in spans(length, longest):
        rows, keys = slice(offset, offset + block), slice(low, offset + block)
        probability, _ = block_probability(
            query_rot[rows, :], key_rot[keys, :], begins[rows, :], offset, low, totals[rows, :]
        )
        grad_block = grads[rows, :]
        value_acc[keys, :] += dot(probability, grad_block, 0, 0)
        row_delta = jnp.sum(
            grad_block.astype(jnp.float32) * low_rows[rows, :].astype(jnp.float32),
            axis=1,
            keepdims=True,
        )
        prob_grad = dot(grad_block, value_low[keys, :], 1, 1)
        score_grad = (
            score_scale * probability.astype(jnp.float32) * (prob_grad - row_delta)
        ).astype(jnp.bfloat16)
        query_acc[rows, :] = dot(score_grad, key_rot[keys, :])
        key_acc[keys, :] += dot(score_grad, query_rot[rows, :], 0, 0)
    parts = []
    for place, source in ((0, query_acc), (1, key_acc)):
        raw = sums[:, place * head_dim : (place + 1) * head_dim]
        gain = gains[place : place + 1, :]
        inv_rms = head_norm(raw, gain)[1]
        cotangent = source[...] * cosine[...] - swap_halves(source[...]) * sine[...]
        low_part, gain_grad = head_norm_back(cotangent, raw, inv_rms, gain)
        parts.append(low_part.astype(jnp.bfloat16))
        gain_out[place : place + 1, :] = gain_grad[None, :]
    parts.append(value_acc[...].astype(jnp.bfloat16))
    for place in range(3):
        slot[:, place * head_dim : (place + 1) * head_dim] = parts[place]


def local_kernel(body, args, outs, scratch=()):
    vmem = pl.BlockSpec(memory_space=pltpu.VMEM)
    return pl.pallas_call(
        body,
        out_shape=outs,
        in_specs=[vmem] * len(args),
        out_specs=[vmem] * len(outs),
        scratch_shapes=list(scratch),
    )(*args)


def pack_slots_kernel(cols, head_dim, query, key, value, out):
    for col in range(cols):
        half = col // 2
        out[col, :, :head_dim] = query[:, col * head_dim : (col + 1) * head_dim]
        for place, source in ((1, key), (2, value)):
            out[col, :, place * head_dim : (place + 1) * head_dim] = source[
                :, half * head_dim : (half + 1) * head_dim
            ]


def pack_wide_kernel(cols, gate, up, out):
    part = gate.shape[1] // cols
    for col in range(cols):
        out[col, :, :part] = gate[:, col * part : (col + 1) * part]
        out[col, :, part:] = up[:, col * part : (col + 1) * part]


def open_wide_kernel(cols, wide, gate, up):
    part = gate.shape[1] // cols
    for col in range(cols):
        gate[:, col * part : (col + 1) * part] = wide[col, :, :part].astype(jnp.float32)
        up[:, col * part : (col + 1) * part] = wide[col, :, part:].astype(jnp.float32)


def open_slots_kernel(cols, head_dim, slots, out):
    for col in range(cols):
        out[:, col * head_dim : (col + 1) * head_dim] = slots[col, :, :head_dim].astype(jnp.float32)
    for half in range(cols // 2):
        for place in (1, 2):
            lanes = slice(place * head_dim, (place + 1) * head_dim)
            begin = (cols + (place - 1) * (cols // 2) + half) * head_dim
            out[:, begin : begin + head_dim] = slots[2 * half, :, lanes].astype(
                jnp.float32
            ) + slots[2 * half + 1, :, lanes].astype(jnp.float32)


MESH = pl.DeviceIdType.MESH


def enter(axes):
    barrier = pltpu.get_barrier_semaphore()
    count = 0
    for axis in axes:
        size, own = lax.axis_size(axis), lax.axis_index(axis)
        for step in range(1, size):
            pl.semaphore_signal(
                barrier, inc=1, device_id={axis: lax.rem(own + step, size)}, device_id_type=MESH
            )
        count += size - 1
    pl.semaphore_wait(barrier, count)


def send(source, target, sems, place, axis, index):
    copy = pltpu.make_async_remote_copy(
        src_ref=source,
        dst_ref=target,
        send_sem=sems[0].at[place],
        recv_sem=sems[1].at[place],
        device_id={axis: index},
        device_id_type=MESH,
    )
    copy.start()
    return copy


def start_swaps(ins, outs, sems):
    cols, own = lax.axis_size("col"), lax.axis_index("col")
    copies = []
    for number in range(len(ins)):
        for step in range(1, cols):
            peer = lax.rem(own + step, cols)
            copies.append(
                send(ins[number].at[peer], outs[number].at[own], sems, (number, step), "col", peer)
            )
        outs[number][own] = ins[number][own]
    return copies


def call_kernel(body, args, outs, scratch, number):
    vmem = pl.BlockSpec(memory_space=pltpu.VMEM)
    return pl.pallas_call(
        body,
        out_shape=outs,
        in_specs=[vmem] * len(args),
        out_specs=[vmem] * len(outs),
        scratch_shapes=scratch,
        compiler_params=pltpu.CompilerParams(collective_id=number, has_side_effects=True),
    )(*args)


def dma(*shape):
    return [pltpu.SemaphoreType.DMA(shape), pltpu.SemaphoreType.DMA(shape)]


def exchange(gathers, swaps, number):
    rows, cols = lax.axis_size("row"), lax.axis_size("col")
    many, total = len(gathers), len(gathers) + len(swaps)

    def body(*refs):
        ins, outs = refs[:total], refs[total : 2 * total]
        sems, swap_sems = refs[2 * total : 2 * total + 2], refs[2 * total + 2 :]
        row, col = lax.axis_index("row"), lax.axis_index("col")
        enter(("row", "col"))
        across, copies = {}, []
        for item in range(many):
            for step in range(1, cols):
                across[item, step] = send(
                    ins[item],
                    outs[item].at[row, col],
                    sems,
                    (item, 0, step),
                    "col",
                    lax.rem(col + step, cols),
                )
        for item in range(many):
            for turn in range(1, rows):
                copies.append(
                    send(
                        ins[item],
                        outs[item].at[row, col],
                        sems,
                        (item, turn, 0),
                        "row",
                        lax.rem(row + turn, rows),
                    )
                )
        copies += start_swaps(ins[many:], outs[many:], swap_sems)
        for item in range(many):
            outs[item][row, col] = ins[item][...]
        for step in range(1, cols):
            origin = lax.rem(col + cols - step, cols)
            for item in range(many):
                across[item, step].wait()
                block = outs[item].at[row, origin]
                for turn in range(1, rows):
                    copies.append(
                        send(
                            block,
                            block,
                            sems,
                            (item, turn, step),
                            "row",
                            lax.rem(row + turn, rows),
                        )
                    )
        for copy in copies:
            copy.wait()

    outs = [jax.ShapeDtypeStruct((rows, cols) + g.shape, g.dtype) for g in gathers]
    outs += [jax.ShapeDtypeStruct(w.shape, w.dtype) for w in swaps]
    scratch = dma(many, rows, cols) + dma(max(len(swaps), 1), cols)
    return call_kernel(body, list(gathers) + list(swaps), outs, scratch, number)


def reduce_rows(partial_value, swaps, number):
    rows, cols = lax.axis_size("row"), lax.axis_size("col")
    local = partial_value.shape[0] // (rows * cols)
    width = partial_value.shape[1]
    shaped = partial_value.astype(jnp.bfloat16).reshape(rows, cols, local, width)
    many = len(swaps)

    def body(*refs):
        part, ins = refs[0], refs[1 : 1 + many]
        result, outs = refs[1 + many], refs[2 + many : 2 + 2 * many]
        first, staged, second = refs[2 + 2 * many : 5 + 2 * many]
        first_sems, second_sems = refs[5 + 2 * many : 7 + 2 * many], refs[7 + 2 * many : 9 + 2 * many]
        swap_sems = refs[9 + 2 * many :]
        row, col = lax.axis_index("row"), lax.axis_index("col")
        enter(("row", "col"))
        down, across = {}, []
        order = list(range(1, cols)) + [0]
        for step in order:
            block = lax.rem(col + step, cols)
            for turn in range(1, rows):
                peer = lax.rem(row + turn, rows)
                down[step, turn] = send(
                    part.at[peer, block],
                    first.at[turn, step],
                    first_sems,
                    (turn, step),
                    "row",
                    peer,
                )
        copies = start_swaps(ins, outs, swap_sems)
        for step in order:
            block = lax.rem(col + step, cols)
            summed = part[row, block].astype(jnp.float32)
            for turn in range(1, rows):
                down[step, turn].wait()
                summed = summed + first[turn, step].astype(jnp.float32)
            if step == 0:
                result[...] = summed
            else:
                staged[step] = summed.astype(jnp.bfloat16)
                across.append(
                    send(staged.at[step], second.at[step], second_sems, (step,), "col", block)
                )
        for step in range(1, cols):
            across[step - 1].wait()
            result[...] += second[step].astype(jnp.float32)
        for copy in copies:
            copy.wait()

    outs = [jax.ShapeDtypeStruct((local, width), jnp.float32)]
    outs += [jax.ShapeDtypeStruct(w.shape, w.dtype) for w in swaps]
    scratch = [
        pltpu.VMEM((rows, cols, local, width), jnp.bfloat16),
        pltpu.VMEM((cols, local, width), jnp.bfloat16),
        pltpu.VMEM((cols, local, width), jnp.bfloat16),
    ]
    scratch += dma(rows, cols) + dma(cols) + dma(max(many, 1), cols)
    return call_kernel(body, [shaped] + list(swaps), outs, scratch, number)


def last_sums(group_value, widths, gains, number):
    sizes = [lax.axis_size(axis) for axis in ("dp", "row", "col")]

    def body(value, gain, *refs):
        value_outs, gain_out = refs[: len(widths)], refs[len(widths)]
        value_in, landed, held = refs[len(widths) + 1 : len(widths) + 4]
        sems = refs[len(widths) + 4 :]
        value_sems, gain_sems = sems[:2], sems[2:]
        enter(("dp", "row", "col"))
        copies, groups = [], lax.axis_size("dp")
        me = lax.axis_index("dp")
        for step in range(1, groups):
            copies.append(
                send(
                    value,
                    value_in.at[step],
                    value_sems,
                    (step,),
                    "dp",
                    lax.rem(me + step, groups),
                )
            )
        held[0] = gain[...]
        for stage, axis in enumerate(("dp", "row", "col")):
            size, own = lax.axis_size(axis), lax.axis_index(axis)
            sent = [
                send(
                    held.at[stage],
                    landed.at[stage, step],
                    gain_sems,
                    (stage, step),
                    axis,
                    lax.rem(own + step, size),
                )
                for step in range(1, size)
            ]
            landed[stage, 0] = held[stage]
            for copy in sent:
                copy.wait()
            total = None
            for place in range(size):
                term = landed[stage, lax.rem(own - place + size, size)]
                total = term if total is None else total + term
            held[stage + 1] = total
        gain_out[...] = held[3]
        for copy in copies:
            copy.wait()
        total = value[...]
        for step in range(1, groups):
            total = total + value_in[step]
        begin = 0
        for size, value_out in zip(widths, value_outs):
            value_out[...] = total[:, begin : begin + size]
            begin += size

    outs = [jax.ShapeDtypeStruct((group_value.shape[0], size), jnp.float32) for size in widths]
    outs.append(jax.ShapeDtypeStruct(gains.shape, jnp.float32))
    scratch = [
        pltpu.VMEM((sizes[0],) + group_value.shape, jnp.float32),
        pltpu.VMEM((3, max(sizes)) + gains.shape, jnp.float32),
        pltpu.VMEM((4,) + gains.shape, jnp.float32),
    ]
    scratch += dma(sizes[0]) + dma(3, max(sizes))
    return call_kernel(body, [group_value, gains], outs, scratch, number)


def dot(left, right, left_dim=1, right_dim=0):
    return lax.dot_general(
        left,
        right,
        (((left_dim,), (right_dim,)), ((), ())),
        preferred_element_type=jnp.float32,
    )


def shards(
    block_input,
    seq_lengths,
    out_grad,
    attn_norm,
    query_weight,
    key_weight,
    value_weight,
    query_norm,
    key_norm,
    out_weight,
    ffn_norm,
    gate_weight,
    up_weight,
    down_weight,
):
    local_rows, width = block_input.shape
    head_dim = query_norm.shape[0]
    col_width = query_weight.shape[0]
    cols = lax.axis_size("col")
    length = local_rows * cols * lax.axis_size("row")
    place = (lax.axis_index("row") * cols + lax.axis_index("col")) * local_rows

    def own_rows(values):
        return lax.dynamic_slice_in_dim(values, place, local_rows, 0)

    out_weight_full = lax.all_gather(out_weight, ("row", "col"), axis=0, tiled=True)

    hidden_width = gate_weight.shape[1] // cols
    (slots,) = local_kernel(
        functools.partial(pack_slots_kernel, cols, head_dim),
        [query_weight, key_weight, value_weight],
        [jax.ShapeDtypeStruct((cols, col_width, 3 * head_dim), jnp.bfloat16)],
    )
    (wide,) = local_kernel(
        functools.partial(pack_wide_kernel, cols),
        [gate_weight, up_weight],
        [jax.ShapeDtypeStruct((cols, col_width, 2 * hidden_width), jnp.bfloat16)],
    )

    input_blocks, slot_blocks = exchange([block_input], [slots], 0)
    input_full = input_blocks.reshape(length, width).astype(jnp.float32)
    slot_weight = slot_blocks.reshape(width, 3 * head_dim)
    first_full = head_norm(input_full, attn_norm)[0].astype(jnp.bfloat16)
    residual = block_input.astype(jnp.float32)
    scale_in = head_norm(residual, attn_norm)[1]
    places = jnp.arange(length, dtype=jnp.int32)
    position = segment_info(seq_lengths[0], length)[1]
    begins = (places - position)[:, None]
    cosine, sine = rope_tables(position, head_dim)
    cosine = jnp.concatenate([cosine, cosine], axis=1)
    sine = jnp.concatenate([-sine, sine], axis=1)
    own_sums = dot(first_full, slot_weight)
    longest = length // 2
    head_gains = jnp.stack([query_norm, key_norm])
    row_shape = jax.ShapeDtypeStruct((length, head_dim), jnp.bfloat16)
    query_rot, key_rot, value_low, attn_low, attn_cols, log_total = local_kernel(
        functools.partial(attend_kernel, longest),
        [own_sums, head_gains, cosine, sine, begins],
        [
            row_shape,
            row_shape,
            row_shape,
            row_shape,
            jax.ShapeDtypeStruct((head_dim, length), jnp.bfloat16),
            jax.ShapeDtypeStruct((length, 1), jnp.float32),
        ],
    )
    cat_blocks, out_blocks, wide_blocks = exchange([attn_cols, out_grad], [wide], 1)
    out_full = out_blocks.reshape(length, width)
    cat_full = cat_blocks.reshape(width, length)
    wide_weight = wide_blocks.reshape(width, 2 * hidden_width)
    middle = input_full + dot(cat_full, out_weight_full, 0, 0)
    normed_mid, scale_mid = head_norm(middle, ffn_norm)
    second_full = normed_mid.astype(jnp.bfloat16)
    wide_sums = dot(second_full, wide_weight)
    gating, upward = wide_sums[:, :hidden_width], wide_sums[:, hidden_width:]
    sigmoid_gate = jax.nn.sigmoid(gating)
    activated = gating * sigmoid_gate
    hidden = (activated * upward).astype(jnp.bfloat16)
    hidden_grad = dot(out_full, down_weight, 1, 1)
    gate_low = (hidden_grad * upward * sigmoid_gate * (1.0 + gating * (1.0 - sigmoid_gate))).astype(
        jnp.bfloat16
    )
    up_low = (hidden_grad * activated).astype(jnp.bfloat16)
    wide_low = jnp.concatenate([gate_low, up_low], axis=1)
    both_parts = [
        dot(wide_low, wide_weight, 1, 1).astype(jnp.bfloat16),
        dot(hidden, down_weight).astype(jnp.bfloat16),
    ]
    (both_sums,) = reduce_rows(jnp.concatenate(both_parts, axis=1), [], 2)
    act_grad2, down_sums = both_sums[:, :width], both_sums[:, width:]
    middle_own = own_rows(middle)
    grad_down = dot(hidden, out_full, 0, 0)
    wide_grad = dot(second_full, wide_low, 0, 0).astype(jnp.bfloat16)
    middle_back, ffn_gain_grad = head_norm_back(
        act_grad2, middle_own, own_rows(scale_mid), ffn_norm
    )
    middle_grad = out_grad.astype(jnp.float32) + middle_back
    middle_blocks, wide_grads = exchange(
        [middle_grad.astype(jnp.bfloat16)],
        [wide_grad.reshape(cols, col_width, 2 * hidden_width)],
        3,
    )
    middle_full = middle_blocks.reshape(length, width)
    grad_outweight = dot(attn_low, middle_full, 0, 0)
    cat_grad = dot(middle_full, out_weight, 1, 1).astype(jnp.bfloat16)
    wide_shape = jax.ShapeDtypeStruct(gate_weight.shape, jnp.float32)
    grad_gate, grad_up = local_kernel(
        functools.partial(open_wide_kernel, cols), [wide_grads], [wide_shape, wide_shape]
    )
    block_output = (middle_own + down_sums).astype(jnp.bfloat16)
    accumulator = pltpu.VMEM((length, head_dim), jnp.float32)
    own_slot, head_gain_grads = local_kernel(
        functools.partial(attend_back_kernel, longest),
        [query_rot, key_rot, value_low, attn_low, log_total, cat_grad]
        + [own_sums, head_gains, cosine, sine, begins],
        [
            jax.ShapeDtypeStruct((length, 3 * head_dim), jnp.bfloat16),
            jax.ShapeDtypeStruct((2, head_dim), jnp.float32),
        ],
        [accumulator] * 3,
    )
    grad_outweight, grad_gate, grad_up, grad_down = lax.psum(
        (grad_outweight, grad_gate, grad_up, grad_down), "dp"
    )
    slot_grad = dot(first_full, own_slot, 0, 0).astype(jnp.bfloat16)
    act_grad1, slot_grads = reduce_rows(
        dot(own_slot, slot_weight, 1, 1),
        [slot_grad.reshape(cols, col_width, 3 * head_dim)],
        4,
    )
    widths = (cols * head_dim, cols // 2 * head_dim, cols // 2 * head_dim)
    (slot_sums,) = local_kernel(
        functools.partial(open_slots_kernel, cols, head_dim),
        [slot_grads],
        [jax.ShapeDtypeStruct((col_width, sum(widths)), jnp.float32)],
    )
    input_back, attn_gain_grad = head_norm_back(act_grad1, residual, scale_in, attn_norm)
    input_grad = middle_grad + input_back
    flat_gains = jnp.concatenate(
        [head_gain_grads.reshape(-1), jnp.zeros((width - 2 * head_dim,), jnp.float32)]
    )
    gains = jnp.stack([attn_gain_grad, ffn_gain_grad, flat_gains])
    gains = jnp.concatenate([gains, jnp.zeros((5, width), jnp.float32)], axis=0)
    grad_query, grad_key, grad_value, gain_sums = last_sums(slot_sums, widths, gains, 5)
    return (
        block_output,
        input_grad,
        gain_sums[0],
        grad_query,
        grad_key,
        grad_value,
        gain_sums[2, :head_dim],
        gain_sums[2, head_dim : 2 * head_dim],
        grad_outweight,
        gain_sums[1],
        grad_gate,
        grad_up,
        grad_down,
    )


def solution(mesh):
    placed = (
        P(("dp", "row", "col"), None),
        P("dp", None),
        P(("dp", "row", "col"), None),
        P(),
        P("col", "row"),
        P("col", "row"),
        P("col", "row"),
        P(),
        P(),
        P(("row", "col"), None),
        P(),
        P("col", "row"),
        P("col", "row"),
        P(("row", "col"), None),
    )
    return jax.shard_map(
        shards,
        mesh=mesh,
        in_specs=placed,
        out_specs=(
            P(("dp", "row", "col"), None),
            P(("dp", "row", "col"), None),
            P(),
            P("col", "row"),
            P("col", "row"),
            P("col", "row"),
            P(),
            P(),
            P(("row", "col"), None),
            P(),
            P("col", "row"),
            P("col", "row"),
            P(("row", "col"), None),
        ),
        check_vma=False,
    )
```
